32 devices in a mesh: field: 4 (over y, x), azim: 8 (over z, core).
Axes of the slice: x: 2, y: 2, z: 4, core: 2. Of those that a mesh axis runs over, the one named last changes fastest.
Arguments:
- scalars: float32 [64, 10, 128, 1024], P('field', None, 'azim'), may hold values from -5 to 5
- wiener: float32 [64, 128, 1024], P('field', 'azim'), may hold values from -1.2 to 1.2
- velocity: float32 [128, 1024], P('azim', 'field'), may hold values from 0.5 to 2
- diffusivity: float32 [128, 1024], P('azim', 'field'), may hold values from 0.1 to 0.8
- mix_rate: float32 [128, 1024], P('azim', 'field'), may hold values from 0.5 to 4
- reaction_rate: float32 [10], replicated, may hold values from 0.2 to 1.5
- equilibrium: float32 [10], replicated, may hold values from -3 to 3
Outputs:
- advanced: float32 [64, 10, 128, 1024], P('field', None, 'azim')
- density: float32 [128, 1024], P('azim', 'field')
The draws below stay inside these ranges and needn't reach their ends.
All inputs are finite; a program needn't handle non-finite values.
Results may differ from the reference program's by a relative error of at most 0.00002.
Values sent between devices are 32-bit elements; how exact they have to be, the bound alone decides.
No kernel may reach another device: no remote copies, remote signals or barrier semaphores. Data moves between devices by JAX's collectives and lax.ppermute only.
A program may use at most 128 MiB of HBM per device.

```python
import math
import jax
import jax.numpy as jnp
from jax import lax

NF = 64
NS = 10
CELLS = 1024
NAZ = 128


def levels(key, dims, pieces, low, top_value):
    factor_of = 1.0
    for dim, blocks in pieces:
        heights = jax.random.uniform(jax.random.fold_in(jax.random.fold_in(key, 6), dim), (blocks,), jnp.float32, low / len(pieces), top_value / len(pieces))
        factor_of = factor_of * jnp.repeat(jnp.exp(heights), dims[dim] // blocks).reshape((-1,) + (1,) * (len(dims) - 1 - dim))
    return factor_of


def noise(rng, shape, spread, bound, shards=(), kind=jnp.bfloat16):
    factor_of = levels(rng, shape, shards, -0.22, 0.18) if shards else 1.0
    values = jax.random.normal(rng, shape, jnp.float32) * spread * factor_of
    return jnp.minimum(jnp.maximum(values, -bound), bound).astype(kind)


def setup_inputs(seed: int = 0) -> dict:
    keys = jax.random.split(jax.random.key(seed), 8)
    return {
        "scalars": noise(keys[0], (NF, NS, NAZ, CELLS), 1.0, 5.0, ((0, 4), (2, 8)), jnp.float32),
        "wiener": noise(keys[1], (NF, NAZ, CELLS), 0.3, 1.2, ((0, 4), (1, 8)), jnp.float32),
        "velocity": jnp.clip(0.5 + 1.5 * jax.random.uniform(keys[2], (NAZ, CELLS), jnp.float32) ** levels(keys[2], (NAZ, CELLS), ((0, 8), (1, 4)), -0.2, 0.2), 0.5, 2.0),
        "diffusivity": jnp.clip(0.1 + 0.7 * jax.random.uniform(keys[3], (NAZ, CELLS), jnp.float32) ** levels(keys[3], (NAZ, CELLS), ((0, 8), (1, 4)), -0.2, 0.2), 0.1, 0.8),
        "mix_rate": jnp.clip(jnp.exp(math.log(4.0) - 2.0794415 * jax.random.uniform(keys[4], (NAZ, CELLS), jnp.float32) ** levels(keys[4], (NAZ, CELLS), ((0, 8), (1, 4)), -0.2, 0.2)), 0.5, 4.0),
        "reaction_rate": jnp.clip(jnp.exp(jax.random.uniform(keys[5], (NS,), jnp.float32, math.log(0.2), math.log(1.5))), 0.2, 1.5),
        "equilibrium": noise(keys[6], (NS,), 1.0, 3.0, (), jnp.float32),
    }


step_size = 0.2

def advance(middle, upper_row, lower_row, velocity, diffusivity, mix_rate, wiener, average, reaction_rate, equilibrium):
    gradient = 0.5 * (upper_row - lower_row)
    laplacian = upper_row - 2.0 * middle + lower_row
    heating = 1.0 + 0.5 * middle[:, 0] * middle[:, 0]
    burning = jnp.exp(1.0 - 1.0 / heating)
    source = reaction_rate[None, :, None, None] * burning[:, None] * (equilibrium[None, :, None, None] - middle)
    tendency = -velocity * gradient + diffusivity * laplacian - 0.5 * mix_rate * (middle - average) + source
    return middle + step_size * tendency + jnp.sqrt(2.0 * diffusivity) * gradient * wiener[:, None]

def run_segment(state, velocity, diffusivity, mix_rate, wiener, reaction_rate, equilibrium):
    average = lax.optimization_barrier(jnp.sum(state, axis=0)) / NF
    upper_row = jnp.roll(state, -1, axis=2)
    lower_row = jnp.roll(state, 1, axis=2)
    return advance(state, upper_row, lower_row, velocity, diffusivity, mix_rate, wiener, average, reaction_rate, equilibrium)

def reference(scalars, wiener, velocity, diffusivity, mix_rate, reaction_rate, equilibrium):
    segment_one = run_segment(scalars, velocity, diffusivity, mix_rate, wiener, reaction_rate, equilibrium)
    advanced = 0.5 * scalars + 0.5 * run_segment(segment_one, velocity, diffusivity, mix_rate, wiener, reaction_rate, equilibrium)
    heating = 1.0 + 0.5 * advanced[:, 0] * advanced[:, 0]
    density = 1.0 / (lax.optimization_barrier(jnp.sum(heating, axis=0)) / NF)
    return (advanced, density)
```

```python
import functools

import jax
import jax.numpy as jnp
from jax import lax
from jax.experimental import pallas as pl
from jax.experimental.pallas import tpu as pltpu
from jax.sharding import PartitionSpec as P

step_size = 0.2
LANES = 128
SUB = 8
F32 = jnp.float32


def ring(count, shift):
    return [(i, (i + shift) % count) for i in range(count)]


def phases(fields):
    return fields.bit_length() - 1


def swap_pairs(fields, slabs, phase):
    bits = phases(fields)
    pairs = []
    for field in range(fields):
        for slab in range(slabs):
            partner = field ^ (1 << ((phase + slab % 2) % bits))
            pairs.append((field * slabs + slab, partner * slabs + slab))
    return pairs


def swap(value, fields, slabs, phase):
    return lax.ppermute(value, ("field", "azim"), swap_pairs(fields, slabs, phase))


def split_rows(value):
    return [value[i : i + SUB] for i in range(0, value.shape[0], SUB)]


def row_index(shape):
    return lax.broadcasted_iota(jnp.int32, shape, 0)


def ups(parts, last, edge):
    turned = [pltpu.roll(part, SUB - 1, 0) for part in parts]
    after = turned[1:] + [edge]
    return [
        turned[i] if after[i] is None else jnp.where(last, after[i], turned[i])
        for i in range(len(parts))
    ]


def downs(parts, first, edge):
    turned = [pltpu.roll(part, 1, 0) for part in parts]
    before = [edge] + turned[:-1]
    return [
        turned[i] if before[i] is None else jnp.where(first, before[i], turned[i])
        for i in range(len(parts))
    ]


def burn(scalar):
    heating = 1.0 + 0.5 * scalar * scalar
    return jnp.exp(1.0 - 1.0 / heating)


def sums_kernel(q_ref, w_ref, sum_ref, noise_ref, mass_ref, burn_ref, lo_ref, lo1_ref, hi_ref, hi1_ref, b_scr):
    F, S, R, width = q_ref.shape
    tiles = R // SUB
    group = S // 2 if S % 2 == 0 else S
    row = row_index((SUB, LANES))
    first, last = row == 0, row == SUB - 1
    zero = jnp.zeros((SUB, LANES), F32)
    for lane in range(0, width, LANES):
        cells = pl.ds(lane, LANES)

        def burning(f, total):
            b = [burn(x) for x in split_rows(q_ref[f, 0, :, cells])]
            for i in range(tiles):
                b_scr[f, pl.ds(i * SUB, SUB), :] = b[i]
            return tuple(t + x for t, x in zip(total, b))

        total = lax.fori_loop(0, F, burning, (zero,) * tiles, unroll=4)
        for i in range(tiles):
            burn_ref[pl.ds(i * SUB, SUB), cells] = total[i]

        for start in range(0, S, group):

            def body(f, carry):
                w = split_rows(w_ref[f, :, cells])
                b = split_rows(b_scr[f])
                out = []
                for g in range(group):
                    q = split_rows(q_ref[f, start + g, :, cells])
                    up, down = ups(q, last, zero), downs(q, first, zero)
                    for i in range(tiles):
                        a, n, m = carry[g * tiles + i]
                        out.append((a + q[i], n + w[i] * (up[i] - down[i]), m + b[i] * q[i]))
                return tuple(out)

            sums = lax.fori_loop(0, F, body, ((zero, zero, zero),) * (group * tiles), unroll=2)
            for g in range(group):
                for i in range(tiles):
                    at = (start + g, pl.ds(i * SUB, SUB), cells)
                    sum_ref[at], noise_ref[at], mass_ref[at] = sums[g * tiles + i]
    for s in range(S):
        rows = pl.ds(s * F, F)
        lo_ref[rows, :] = q_ref[:, s, 0, :]
        lo1_ref[rows, :] = q_ref[:, s, 1, :]
        hi_ref[rows, :] = q_ref[:, s, R - 1, :]
        hi1_ref[rows, :] = q_ref[:, s, R - 2, :]


def field_sums(q, w, width):
    F, S, R, N = q.shape
    cube = jax.ShapeDtypeStruct((S, R, N), F32)
    rows = jax.ShapeDtypeStruct((S * F, N), F32)
    cube_spec = pl.BlockSpec((S, R, width), lambda c: (0, 0, c))
    rows_spec = pl.BlockSpec((S * F, width), lambda c: (0, c))
    return pl.pallas_call(
        sums_kernel,
        grid=(N // width,),
        in_specs=[
            pl.BlockSpec((F, S, R, width), lambda c: (0, 0, 0, c)),
            pl.BlockSpec((F, R, width), lambda c: (0, 0, c)),
        ],
        out_specs=[cube_spec] * 3 + [pl.BlockSpec((R, width), lambda c: (0, c))] + [rows_spec] * 4,
        out_shape=[cube] * 3 + [jax.ShapeDtypeStruct((R, N), F32)] + [rows] * 4,
        scratch_shapes=[pltpu.VMEM((F, R, LANES), F32)],
        compiler_params=pltpu.CompilerParams(vmem_limit_bytes=24 << 20),
        name="sums",
    )(q, w)


def rim_kernel(
    order_ref, rate_ref, goal_ref, gas_ref, sum_ref, noise_ref, mass_ref, burn_ref, lo_ref, lo1_ref,
    hi_ref, hi1_ref, below_ref, above_ref, w_ref,
    total_ref, send_lo_ref, send_hi_ref, coef_ref, edge_ref,
):
    del order_ref
    S, R, width = sum_ref.shape
    F = w_ref.shape[0]
    velocity, diffusivity, mix_rate = gas_ref[0, 0], gas_ref[0, 1], gas_ref[0, 2]
    half = 0.5 * jnp.sqrt(2.0 * diffusivity)
    up_coef = step_size * diffusivity - (0.5 * step_size) * velocity
    down_coef = step_size * diffusivity + (0.5 * step_size) * velocity
    keep = 1.0 - (2.0 * step_size) * diffusivity
    mix = (0.5 * step_size) * mix_rate
    own = keep - mix
    coef_ref[0] = up_coef
    coef_ref[1] = down_coef
    coef_ref[2] = own
    coef_ref[3] = half
    coef_ref[4] = mix
    first_row, last_row = pl.ds(0, 1), pl.ds(R - 1, 1)
    w_lo, w_hi = w_ref[:, 0, :], w_ref[:, R - 1, :]

    def at(value, r):
        return value[r : r + 1]

    lo_up = at(up_coef, 0) + at(half, 0) * w_lo
    lo_down = at(down_coef, 0) - at(half, 0) * w_lo
    hi_up = at(up_coef, R - 1) + at(half, R - 1) * w_hi
    hi_down = at(down_coef, R - 1) - at(half, R - 1) * w_hi
    edge_ref[0] = 0.5 * lo_down
    edge_ref[1] = 0.5 * hi_up
    lo_burn = step_size * burn(lo_ref[pl.ds(0, F), :])
    hi_burn = step_size * burn(hi_ref[pl.ds(0, F), :])
    row = row_index((R, width))
    first, last = row == 0, row == R - 1
    burned = burn_ref[...]
    for s in range(S):
        rows = pl.ds(s * F, F)
        rate, goal = rate_ref[s], goal_ref[s]
        below, above = below_ref[rows, :], above_ref[rows, :]
        q_lo, q_hi = lo_ref[rows, :], hi_ref[rows, :]
        send_lo_ref[rows, :] = (
            at(own, 0) * q_lo
            + lo_up * lo1_ref[rows, :]
            + lo_down * below
            + (rate * lo_burn) * (goal - q_lo)
        )
        send_hi_ref[rows, :] = (
            at(own, R - 1) * q_hi
            + hi_up * above
            + hi_down * hi1_ref[rows, :]
            + (rate * hi_burn) * (goal - q_hi)
        )
        sum_below = jnp.sum(below, axis=0, keepdims=True)
        sum_above = jnp.sum(above, axis=0, keepdims=True)
        noise_below = jnp.sum(w_lo * below, axis=0, keepdims=True)
        noise_above = jnp.sum(w_hi * above, axis=0, keepdims=True)
        total_ref[pl.ds(S * R + s, 1), :] = sum_below
        total_ref[pl.ds(S * R + S + s, 1), :] = sum_above
        middle = sum_ref[s]
        upper = jnp.where(last, sum_above, pltpu.roll(middle, R - 1, 0))
        lower = jnp.where(first, sum_below, pltpu.roll(middle, 1, 0))
        noise = noise_ref[s] + jnp.where(last, noise_above, 0.0) - jnp.where(first, noise_below, 0.0)
        total_ref[pl.ds(s * R, R), :] = (
            keep * middle
            + up_coef * upper
            + down_coef * lower
            + half * noise
            + (step_size * rate) * (goal * burned - mass_ref[s])
        )
    send_lo_ref[pl.ds(S * F, SUB), :] = jnp.broadcast_to(at(mix, 0), (SUB, width))
    send_hi_ref[pl.ds(S * F, SUB), :] = jnp.broadcast_to(at(mix, R - 1), (SUB, width))
    tail = total_ref.shape[0] - (S * R + 2 * S)
    if tail:
        total_ref[pl.ds(S * R + 2 * S, tail), :] = jnp.zeros((tail, width), F32)


def rim(order, rate, goal, gas, sums, packed, below, above, w):
    total, noise, mass, burned = sums
    S, R, N = total.shape
    F = w.shape[0]
    width = gas.shape[-1]
    height = -(-(S * R + 2 * S) // SUB) * SUB
    cube_spec = pl.BlockSpec((S, R, width), lambda c, o: (0, 0, c))
    rows_spec = pl.BlockSpec((S * F, width), lambda c, o: (0, c))
    send_spec = pl.BlockSpec((S * F + SUB, width), lambda c, o: (0, c))
    smem = pl.BlockSpec(memory_space=pltpu.SMEM)
    return pl.pallas_call(
        rim_kernel,
        grid_spec=pltpu.PrefetchScalarGridSpec(
            num_scalar_prefetch=1,
            grid=(N // width,),
            in_specs=[smem, smem, pl.BlockSpec((1, 3, R, width), lambda c, o: (o[c], 0, 0, 0))]
            + [cube_spec] * 3
            + [pl.BlockSpec((R, width), lambda c, o: (0, c))]
            + [rows_spec] * 6
            + [pl.BlockSpec((F, R, width), lambda c, o: (0, 0, c))],
            out_specs=[
                pl.BlockSpec((height, width), lambda c, o: (0, c)),
                send_spec,
                send_spec,
                pl.BlockSpec((5, R, width), lambda c, o: (0, 0, c)),
                pl.BlockSpec((2, F, width), lambda c, o: (0, 0, c)),
            ],
        ),
        out_shape=[
            jax.ShapeDtypeStruct((height, N), F32),
            jax.ShapeDtypeStruct((S * F + SUB, N), F32),
            jax.ShapeDtypeStruct((S * F + SUB, N), F32),
            jax.ShapeDtypeStruct((5, R, N), F32),
            jax.ShapeDtypeStruct((2, F, N), F32),
        ],
        compiler_params=pltpu.CompilerParams(vmem_limit_bytes=24 << 20),
        name="rim",
    )(order, rate, goal, gas, total, noise, mass, burned, *packed, below, above, w)


def segments_kernel(
    count, rate_ref, goal_ref, q_ref, w_ref, coef_ref, sum_ref, got_ref, below_ref, above_ref, out_ref,
    pull_scr, edge_scr,
):
    F, S, R, width = q_ref.shape
    tiles = R // SUB
    row = row_index((SUB, LANES))
    first, last = row == 0, row == SUB - 1
    for s in range(S):
        pull_scr[s] = (coef_ref[4] * (1.0 / count)) * (sum_ref[s] + got_ref[s])
    for lane in range(width // LANES):
        for i, ref in enumerate((below_ref, above_ref)):
            edge_scr[i, lane] = ref[:, pl.ds(lane * LANES, LANES)]

    def tile(step, carry):
        lane, f = step // F, step % F
        cells = pl.ds(pl.multiple_of(lane * LANES, LANES), LANES)
        up_coef, down_coef, own, half = (split_rows(coef_ref[i, :, cells]) for i in range(4))
        w = split_rows(w_ref[f, :, cells])
        kick = [h * x for h, x in zip(half, w)]
        rise = [c + k for c, k in zip(up_coef, kick)]
        fall = [c - k for c, k in zip(down_coef, kick)]
        rise_in = rise[:-1] + [jnp.where(last, 0.0, rise[-1])]
        fall_in = [jnp.where(first, 0.0, fall[0])] + fall[1:]
        hot = None
        hot_next = None
        for s in range(S):
            rate, goal = step_size * rate_ref[s], goal_ref[s]
            q = split_rows(q_ref[f, s, :, cells])
            pull = split_rows(pull_scr[s, :, cells])
            below, above = (
                jnp.broadcast_to(edge_scr[i, lane, pl.ds(s * F + f, 1), :], (SUB, LANES)) for i in range(2)
            )
            up, down = ups(q, last, above), downs(q, first, below)
            if s == 0:
                hot = [burn(x) for x in q]
            one = [
                own[i] * q[i] + rise[i] * up[i] + fall[i] * down[i] + pull[i] + (rate * hot[i]) * (goal - q[i])
                for i in range(tiles)
            ]
            if s == 0:
                hot_next = [burn(x) for x in one]
            up, down = ups(one, last, None), downs(one, first, None)
            for i in range(tiles):
                two = (
                    own[i] * one[i]
                    + rise_in[i] * up[i]
                    + fall_in[i] * down[i]
                    + (rate * hot_next[i]) * (goal - one[i])
                )
                out_ref[f, s, pl.ds(i * SUB, SUB), cells] = 0.5 * (q[i] + two)
        return carry

    lax.fori_loop(0, F * (width // LANES), tile, 0)


def segments(count, rate, goal, q, w, coef, total, got, below, above, width):
    F, S, R, N = q.shape
    big = pl.BlockSpec((F, S, R, width), lambda c: (0, 0, 0, c))
    cube_spec = pl.BlockSpec((S, R, width), lambda c: (0, 0, c))
    rows_spec = pl.BlockSpec((S * F, width), lambda c: (0, c))
    smem = pl.BlockSpec(memory_space=pltpu.SMEM)
    return pl.pallas_call(
        functools.partial(segments_kernel, count),
        grid=(N // width,),
        in_specs=[
            smem,
            smem,
            big,
            pl.BlockSpec((F, R, width), lambda c: (0, 0, c)),
            pl.BlockSpec((5, R, width), lambda c: (0, 0, c)),
            cube_spec,
            cube_spec,
            rows_spec,
            rows_spec,
        ],
        out_specs=big,
        out_shape=jax.ShapeDtypeStruct((F, S, R, N), F32),
        scratch_shapes=[
            pltpu.VMEM((S, R, width), F32),
            pltpu.VMEM((2, width // LANES, S * F, LANES), F32),
        ],
        compiler_params=pltpu.CompilerParams(vmem_limit_bytes=24 << 20),
        name="segments",
    )(rate, goal, q, w, coef, total, got, below, above)


def edge_rows(count, scalars, R, total_ref, got_ref, edge_ref, sides, add_scr):
    F, N = edge_ref.shape[1:]
    S = (sides[0].shape[0] - SUB) // F
    for i, ref in enumerate(sides):
        mix = ref[pl.ds(S * F, 1), :] * (1.0 / count)
        for j, s in enumerate(scalars):
            at = pl.ds(S * R + i * S + s, 1)
            value = edge_ref[i] * (ref[pl.ds(s * F, F), :] + mix * (total_ref[at, :] + got_ref[at, :]))
            for lane in range(N // LANES):
                add_scr[i, j, lane] = value[:, lane * LANES : (lane + 1) * LANES]


def finish_scalar(count, s, j, c_ref, total_ref, got_ref, coef_ref, out_ref, add_scr, heat_ref=None):
    F, _, R, N = c_ref.shape
    row = row_index((SUB, LANES))
    first, last = row == 0, row == SUB - 1
    rows = pl.ds(pl.multiple_of(s * R, R), R)
    for lane in range(N // LANES):
        cells = pl.ds(lane * LANES, LANES)
        pull = split_rows(coef_ref[4, :, cells] * (0.5 / count) * (total_ref[rows, cells] + got_ref[rows, cells]))

        def body(f, heat):
            add_lo, add_hi = (
                jnp.broadcast_to(add_scr[i, j, lane, pl.ds(f, 1), :], (SUB, LANES)) for i in range(2)
            )
            value = [x + p for x, p in zip(split_rows(c_ref[f, 0, :, cells]), pull)]
            value[0] = value[0] + jnp.where(first, add_lo, 0.0)
            value[-1] = value[-1] + jnp.where(last, add_hi, 0.0)
            for i, x in enumerate(value):
                out_ref[f, 0, pl.ds(i * SUB, SUB), cells] = x
            return tuple(h + 0.5 * x * x for h, x in zip(heat, value)) if heat else heat

        start = () if heat_ref is None else (jnp.full((SUB, LANES), float(F), F32),) * len(pull)
        heat = lax.fori_loop(0, F, body, start, unroll=4)
        for i, h in enumerate(heat):
            heat_ref[pl.ds(i * SUB, SUB), cells] = h


def head_kernel(count, c_ref, total_ref, got_ref, coef_ref, edge_ref, lo_ref, hi_ref, out_ref, heat_ref, add_scr):
    edge_rows(count, [0], c_ref.shape[2], total_ref, got_ref, edge_ref, (lo_ref, hi_ref), add_scr)
    finish_scalar(count, 0, 0, c_ref, total_ref, got_ref, coef_ref, out_ref, add_scr, heat_ref)


def rest_kernel(count, first_out_ref, c_ref, total_ref, got_ref, coef_ref, edge_ref, lo_ref, hi_ref, out_ref, add_scr):
    del first_out_ref
    step = pl.program_id(0)

    @pl.when(step == 0)
    def _():
        scalars = range(1, 1 + add_scr.shape[1])
        edge_rows(count, scalars, c_ref.shape[2], total_ref, got_ref, edge_ref, (lo_ref, hi_ref), add_scr)

    finish_scalar(count, step + 1, step, c_ref, total_ref, got_ref, coef_ref, out_ref, add_scr)


def finish(count, c, total, got, coef, edge, lo, hi):
    F, S, R, N = c.shape

    def whole(value):
        return pl.BlockSpec(value.shape, lambda *_: (0,) * value.ndim)

    small = (total, got, coef, edge, lo, hi)
    params = pltpu.CompilerParams(vmem_limit_bytes=24 << 20)

    def scratch(scalars):
        return [pltpu.VMEM((2, scalars, N // LANES, F, LANES), F32)]

    out_shape = jax.ShapeDtypeStruct((F, S, R, N), F32)
    at_zero = pl.BlockSpec((F, 1, R, N), lambda g: (0, 0, 0, 0))
    at_next = pl.BlockSpec((F, 1, R, N), lambda g: (0, g + 1, 0, 0))
    partial, heat = pl.pallas_call(
        functools.partial(head_kernel, count),
        grid=(1,),
        in_specs=[at_zero] + [whole(x) for x in small],
        out_specs=[at_zero, pl.BlockSpec((R, N), lambda g: (0, 0))],
        out_shape=[out_shape, jax.ShapeDtypeStruct((R, N), F32)],
        scratch_shapes=scratch(1),
        compiler_params=params,
        name="head",
    )(c, *small)
    advanced = pl.pallas_call(
        functools.partial(rest_kernel, count),
        grid=(S - 1,),
        in_specs=[pl.BlockSpec(memory_space=pl.ANY), at_next] + [whole(x) for x in small],
        out_specs=at_next,
        out_shape=out_shape,
        scratch_shapes=scratch(S - 1),
        input_output_aliases={0: 0},
        compiler_params=params,
        name="rest",
    )(partial, c, *small)
    return advanced, heat


def shards(fields, slabs, scalars, wiener, velocity, diffusivity, mix_rate, reaction_rate, equilibrium):
    bits = phases(fields)
    F, S, R, N = scalars.shape
    count = float(F * fields)
    me, slab = lax.axis_index("field"), lax.axis_index("azim")

    gas = jnp.stack([velocity, diffusivity, mix_rate])[None]
    order = jnp.zeros((fields,), jnp.int32)
    away = jnp.arange(fields, dtype=jnp.int32) ^ me
    for phase in range(bits):
        gas = jnp.concatenate([gas, swap(gas, fields, slabs, phase)])
        bit = (phase + slab % 2) % bits
        order = order | (((away >> bit) & 1) << phase)

    *sums, lo, lo1, hi, hi1 = field_sums(scalars, wiener, 2 * LANES)
    below = lax.ppermute(hi, "azim", ring(slabs, 1))
    above = lax.ppermute(lo, "azim", ring(slabs, -1))

    total, got = sums[0], None
    for phase in range(bits):
        total = total if got is None else total + got
        got = swap(total, fields, slabs, phase)

    later, send_lo, send_hi, coef, edge = rim(
        order, reaction_rate, equilibrium, gas, sums, (lo, lo1, hi, hi1), below, above, wiener
    )
    next_lo = lax.ppermute(send_hi, "azim", ring(slabs, 1))
    next_hi = lax.ppermute(send_lo, "azim", ring(slabs, -1))

    later_got = None
    for phase in range(bits):
        later = later if later_got is None else later + later_got
        later_got = swap(later, fields, slabs, phase)

    c = segments(
        count, reaction_rate, equilibrium, scalars, wiener, coef, total, got, below, above, 2 * LANES
    )
    advanced, heat = finish(count, c, later, later_got, coef, edge, next_lo, next_hi)
    for phase in range(bits):
        heat = heat + swap(heat, fields, slabs, phase)
    mine = lax.dynamic_slice_in_dim(heat, me * (N // fields), N // fields, axis=1)
    return advanced, 1.0 / (mine / count)


def solution(mesh):
    return jax.shard_map(
        functools.partial(shards, mesh.shape["field"], mesh.shape["azim"]),
        mesh=mesh,
        in_specs=(
            P("field", None, "azim", None),
            P("field", "azim", None),
            P("azim", "field"),
            P("azim", "field"),
            P("azim", "field"),
            P(),
            P(),
        ),
        out_specs=(P("field", None, "azim", None), P("azim", "field")),
        check_vma=False,
    )
```
